32 devices in a mesh: groups: 2 (over y), nodes: 16 (over z, x, core).
Axes of the slice: x: 2, y: 2, z: 4, core: 2. Of those that a mesh axis runs over, the one named last changes fastest.
Arguments:
- grid: bfloat16 [4096, 512], P(('groups', 'nodes')), parts along dimension 0, may hold values from -6 to 6
- hidden: bfloat16 [8192, 512], P(('groups', 'nodes')), parts along dimension 0, may hold values from -6 to 6
- enc_nbr: int32 [4096, 32], P('nodes'), may hold values from 0 to 2047, as said below
- dec_nbr: int32 [2048, 3], P('nodes'), may hold values from 0 to 4095, as said below
- enc_qkv: bfloat16 [512, 1536], replicated, may hold values from -0.25 to 0.25
- enc_out: bfloat16 [512, 512], replicated, may hold values from -0.25 to 0.25
- proc_qkv: bfloat16 [512, 1536], replicated, may hold values from -0.25 to 0.25
- proc_out: bfloat16 [512, 512], replicated, may hold values from -0.25 to 0.25
- dec_qkv: bfloat16 [512, 1536], replicated, may hold values from -0.25 to 0.25
- dec_out: bfloat16 [512, 512], replicated, may hold values from -0.25 to 0.25
- mlp_in: bfloat16 [512, 2048], replicated, may hold values from -0.25 to 0.25
- mlp_out: bfloat16 [2048, 512], replicated, may hold values from -0.125 to 0.125
Outputs:
- grid_out: bfloat16 [4096, 512], P(('groups', 'nodes')), parts along dimension 0
- hidden_two: bfloat16 [8192, 512], P(('groups', 'nodes')), parts along dimension 0
The draws below stay inside these ranges and needn't reach their ends.
There are 2 independent parts, one for each index of `groups`. The reference program is written for one: setup_inputs(seed, part) draws one part's arguments, and reference() takes and returns one part's arrays. A program takes and returns all parts, laid end to end along the dimension named above; an argument that names none is the same for every part. Nothing has to cross between parts.
Inputs may be any that keep to these rules, and one draw needn't show every extreme that they name: `enc_nbr`: row i names grid nodes of regions r - 1 to r + 1 only, with r = i // 256, region r holding grid nodes r * 128 to (r + 1) * 128 - 1. `dec_nbr`: row i names hidden nodes of regions r - 1 to r + 1 only, with r = i // 128, region r holding hidden nodes r * 256 to (r + 1) * 256 - 1.
All inputs are finite; a program needn't handle non-finite values.
Results may differ from the reference program's by a relative error of at most 0.015.
Values may be sent and summed in bfloat16 or wider, within the bound.
A program may use at most 64 MiB of HBM per device.

```python
import jax
import jax.numpy as jnp
from jax import lax

D = 512
HEADS = 16
FF = 2048
GRID_DEV = 128
HID_DEV = 256
WIN = 512
K_ENC = 32
K_DEC = 3
GRID = 2048
HIDDEN_SIZE = 4096
N_NODES = 16


def near_lists(key, row_total, row_block, target_block, slot_count):
    region = jnp.arange(row_total, dtype=jnp.int32) // row_block
    lower_edge = jnp.maximum(region - 1, 0) * target_block
    upper_edge = jnp.minimum(region + 2, N_NODES) * target_block
    drawn_bits = jax.random.randint(key, (row_total, slot_count), 0, 1 << 30, dtype=jnp.int32)
    return lower_edge[:, None] + drawn_bits % (upper_edge - lower_edge)[:, None]


def draw_enc_nbr(key, part):
    return near_lists(jax.random.fold_in(key, 11), HIDDEN_SIZE, HID_DEV, GRID_DEV, K_ENC)


def draw_dec_nbr(key, part):
    return near_lists(jax.random.fold_in(key, 23), GRID, GRID_DEV, HID_DEV, K_DEC)


def block_levels(stream_key, shape, cuts, least, top_value):
    gain = 1.0
    for dim, shards_of in cuts:
        heights = jax.random.uniform(jax.random.fold_in(jax.random.fold_in(stream_key, 6), dim), (shards_of,), jnp.float32, least / len(cuts), top_value / len(cuts))
        gain = gain * jnp.repeat(jnp.exp(heights), shape[dim] // shards_of).reshape((-1,) + (1,) * (len(shape) - 1 - dim))
    return gain


def bell_draw(key, extent, width, reach, cuts=(), kind=jnp.bfloat16):
    gain = block_levels(key, extent, cuts, -0.22, 0.18) if cuts else 1.0
    array = jax.random.normal(key, extent, jnp.float32) * width * gain
    return jnp.minimum(jnp.maximum(array, -reach), reach).astype(kind)


def setup_inputs(seed: int = 0, part: int = 0) -> dict:
    key_list = jax.random.split(jax.random.key(seed), 13)
    part_keys = jax.random.split(jax.random.fold_in(key_list[12], part), 13)
    return {
        "grid": bell_draw(part_keys[0], (GRID, D), 1.0, 6.0, ((0, 16),)),
        "hidden": bell_draw(part_keys[1], (HIDDEN_SIZE, D), 1.0, 6.0, ((0, 16),)),
        "enc_nbr": draw_enc_nbr(jax.random.fold_in(key_list[12], 71), part),
        "dec_nbr": draw_dec_nbr(jax.random.fold_in(key_list[12], 71), part),
        "enc_qkv": bell_draw(key_list[4], (D, 3 * D), D ** -0.5, 0.25),
        "enc_out": bell_draw(key_list[5], (D, D), D ** -0.5, 0.25),
        "proc_qkv": bell_draw(key_list[6], (D, 3 * D), D ** -0.5, 0.25),
        "proc_out": bell_draw(key_list[7], (D, D), D ** -0.5, 0.25),
        "dec_qkv": bell_draw(key_list[8], (D, 3 * D), D ** -0.5, 0.25),
        "dec_out": bell_draw(key_list[9], (D, D), D ** -0.5, 0.25),
        "mlp_in": bell_draw(key_list[10], (D, FF), D ** -0.5, 0.25),
        "mlp_out": bell_draw(key_list[11], (FF, D), FF ** -0.5, 0.125),
    }


EPSILON = 1e-05

def layer_norm(values):
    values = values.astype(jnp.float32)
    center = values - lax.optimization_barrier(jnp.mean(values, axis=-1, keepdims=True))
    spread = lax.optimization_barrier(jnp.mean(center * center, axis=-1, keepdims=True))
    return (center * lax.rsqrt(spread + EPSILON)).astype(jnp.bfloat16)

def neighbour_attend(queries, key_values):
    row_count = queries.shape[0]
    slot_count = key_values.shape[1]
    model_width = queries.shape[1]
    head_size = model_width // HEADS
    query_heads = queries.astype(jnp.float32).reshape(row_count, HEADS, head_size)
    key_heads = key_values[:, :, :model_width].astype(jnp.float32).reshape(row_count, slot_count, HEADS, head_size)
    value_heads = key_values[:, :, model_width:].astype(jnp.float32).reshape(row_count, slot_count, HEADS, head_size)
    scores = jnp.einsum('nhd,nkhd->nhk', query_heads, key_heads) / jnp.sqrt(jnp.float32(head_size))
    weights = jax.nn.softmax(scores, axis=-1)
    return jnp.einsum('nhk,nkhd->nhd', weights, value_heads).reshape(row_count, model_width)

def window_attend(queries, key_values):
    row_count = queries.shape[0]
    key_count = key_values.shape[0]
    model_width = queries.shape[1]
    head_size = model_width // HEADS
    query_heads = queries.astype(jnp.float32).reshape(row_count, HEADS, head_size)
    key_heads = key_values[:, :model_width].astype(jnp.float32).reshape(key_count, HEADS, head_size)
    value_heads = key_values[:, model_width:].astype(jnp.float32).reshape(key_count, HEADS, head_size)
    scores = jnp.einsum('nhd,whd->hnw', query_heads, key_heads) / jnp.sqrt(jnp.float32(head_size))
    weights = jax.nn.softmax(scores, axis=-1)
    return jnp.einsum('hnw,whd->nhd', weights, value_heads).reshape(row_count, model_width)

def product(left, right):
    return jnp.dot(left, right, preferred_element_type=jnp.float32)

def reference(grid, hidden, enc_nbr, dec_nbr, enc_qkv, enc_out, proc_qkv, proc_out, dec_qkv, dec_out, mlp_in, mlp_out):
    model_width = grid.shape[1]
    grid_normed = layer_norm(grid)
    enc_queries = product(layer_norm(hidden), enc_qkv[:, :model_width]).astype(jnp.bfloat16)
    enc_pairs = product(grid_normed, enc_qkv[:, model_width:]).astype(jnp.bfloat16)

    def encode_block(inputs):
        block_queries, block_lists = inputs
        return neighbour_attend(block_queries, enc_pairs[block_lists]).astype(jnp.bfloat16)
    hidden_blocks = HIDDEN_SIZE // HID_DEV
    enc_mix = lax.map(encode_block, (enc_queries.reshape(hidden_blocks, HID_DEV, model_width), enc_nbr.reshape(hidden_blocks, HID_DEV, K_ENC))).reshape(HIDDEN_SIZE, model_width)
    hidden_one = (hidden.astype(jnp.float32) + product(enc_mix, enc_out)).astype(jnp.bfloat16)
    proc_all = product(layer_norm(hidden_one), proc_qkv).astype(jnp.bfloat16)

    def process_window(window_rows):
        return window_attend(window_rows[:, :model_width], window_rows[:, model_width:]).astype(jnp.bfloat16)
    proc_mix = lax.map(process_window, proc_all.reshape(HIDDEN_SIZE // WIN, WIN, 3 * model_width)).reshape(HIDDEN_SIZE, model_width)
    hidden_two = (hidden_one.astype(jnp.float32) + product(proc_mix, proc_out)).astype(jnp.bfloat16)
    dec_pairs = product(layer_norm(hidden_two), dec_qkv[:, model_width:]).astype(jnp.bfloat16)
    dec_queries = product(grid_normed, dec_qkv[:, :model_width]).astype(jnp.bfloat16)

    def decode_block(inputs):
        block_queries, block_lists = inputs
        return neighbour_attend(block_queries, dec_pairs[block_lists]).astype(jnp.bfloat16)
    grid_blocks = GRID // GRID_DEV
    dec_mix = lax.map(decode_block, (dec_queries.reshape(grid_blocks, GRID_DEV, model_width), dec_nbr.reshape(grid_blocks, GRID_DEV, K_DEC))).reshape(GRID, model_width)
    grid_one = (grid.astype(jnp.float32) + product(dec_mix, dec_out)).astype(jnp.bfloat16)
    mlp_hidden = jax.nn.gelu(product(layer_norm(grid_one), mlp_in)).astype(jnp.bfloat16)
    grid_out = (grid_one.astype(jnp.float32) + product(mlp_hidden, mlp_out)).astype(jnp.bfloat16)
    return (grid_out, hidden_two)
```

```python
import functools
import math

import jax
import jax.numpy as jnp
from jax import lax
from jax.experimental import pallas as pl
from jax.experimental.pallas import tpu as pltpu
from jax.sharding import PartitionSpec as P

HEADS = 16
EPSILON = 1e-05
LANES = 128
CHUNKS = 2
F32 = jnp.float32
BF16 = jnp.bfloat16
MESH = pl.DeviceIdType.MESH


def layer_norm(values):
    values = values.astype(F32)
    center = values - jnp.mean(values, axis=-1, keepdims=True)
    spread = jnp.mean(center * center, axis=-1, keepdims=True)
    return (center * lax.rsqrt(spread + EPSILON)).astype(BF16)


def product(left, right):
    return jnp.dot(left, right, preferred_element_type=F32)


def scores_of(left, right):
    return lax.dot_general(left, right, (((1,), (1,)), ((), ())), preferred_element_type=F32)


def head_masks(rows, head_size):
    lane = lax.broadcasted_iota(jnp.int32, (rows, LANES), 1)
    return [lane // head_size == h for h in range(LANES // head_size)]


def attend_group(queries, keys, values_ext, bias, masks):
    rows = queries.shape[0]
    stacked = jnp.concatenate([jnp.where(m, queries, jnp.zeros_like(queries)) for m in masks], axis=0)
    scores = scores_of(stacked, keys)
    if bias is not None:
        scores = (scores.reshape(len(masks), rows, -1) + bias[None]).reshape(scores.shape)
    maxima = jnp.max(scores, axis=-1, keepdims=True)
    weights = jnp.exp2(scores - maxima).astype(BF16)
    mixed = product(weights, values_ext)
    num = mixed[:rows, :LANES]
    den = mixed[:rows, LANES:]
    for h in range(1, len(masks)):
        part = mixed[h * rows : (h + 1) * rows]
        num = jnp.where(masks[h], part[:, :LANES], num)
        den = jnp.where(masks[h], part[:, LANES:], den)
    return num / den


def kernel(
    n,
    grid_hbm, hidden_hbm, enc_nbr_hbm, dec_nbr_hbm,
    enc_qkv_hbm, enc_out_hbm, proc_qkv_hbm, proc_out_hbm,
    dec_qkv_hbm, dec_out_hbm, mlp_in_hbm, mlp_out_hbm,
    grid_out_hbm, hidden_out_hbm,
    grid, hidden, enc_nbr, dec_nbr,
    enc_qkv, enc_out, proc_qkv, proc_out, dec_qkv, dec_out, mlp_in, mlp_out,
    grid_out, hidden_out,
    grid_l, grid_r, bias, enc_q, enc_k, enc_v,
    hidden_one, norm_one, norm_far, proc_q, proc_k, proc_v,
    norm_two, two_l, two_r, mix,
    load_sem, store_sem, send_sem, recv_sem,
):
    me = lax.axis_index("nodes")
    far = me + 1 - 2 * (me % 2)
    has_l = me > 0
    has_r = me < n - 1
    gb, width = grid.shape
    hb = hidden.shape[0]
    head_size = width // HEADS
    groups = width // LANES
    rows = hb // CHUNKS
    scale = math.log2(math.e) / math.sqrt(head_size)

    barrier = pltpu.get_barrier_semaphore()

    @pl.when(has_l)
    def _():
        pl.semaphore_signal(barrier, inc=1, device_id={"nodes": me - 1}, device_id_type=MESH)

    @pl.when(has_r)
    def _():
        pl.semaphore_signal(barrier, inc=1, device_id={"nodes": me + 1}, device_id_type=MESH)

    pairs = [
        (grid_hbm, grid), (hidden_hbm, hidden), (enc_nbr_hbm, enc_nbr), (enc_qkv_hbm, enc_qkv),
        (dec_nbr_hbm, dec_nbr), (enc_out_hbm, enc_out), (proc_qkv_hbm, proc_qkv), (proc_out_hbm, proc_out),
        (dec_qkv_hbm, dec_qkv), (dec_out_hbm, dec_out), (mlp_in_hbm, mlp_in), (mlp_out_hbm, mlp_out),
    ]
    loads = [pltpu.make_async_copy(s, d, load_sem.at[i]) for i, (s, d) in enumerate(pairs)]
    (ld_grid, ld_hidden, ld_enbr, ld_eqkv, ld_dnbr, ld_eout, ld_pqkv, ld_pout, ld_dqkv, ld_dout, ld_min, ld_mout) = loads
    for ld in (ld_grid, ld_hidden, ld_enbr, ld_eqkv):
        ld.start()

    def remote(src, dst, k, to):
        return pltpu.make_async_remote_copy(
            src_ref=src, dst_ref=dst, send_sem=send_sem.at[k], recv_sem=recv_sem.at[k],
            device_id={"nodes": to}, device_id_type=MESH,
        )

    grid_up = remote(grid_hbm, grid_l, 0, me + 1)
    grid_down = remote(grid_hbm, grid_r, 1, me - 1)

    pl.semaphore_wait(barrier, jnp.where(has_l, 1, 0) + jnp.where(has_r, 1, 0))

    @pl.when(has_r)
    def _():
        grid_up.start()

    @pl.when(has_l)
    def _():
        grid_down.start()

    @pl.when(jnp.logical_not(has_l))
    def _():
        grid_l[...] = jnp.zeros_like(grid_l)
        two_l[...] = jnp.zeros_like(two_l)

    @pl.when(jnp.logical_not(has_r))
    def _():
        grid_r[...] = jnp.zeros_like(grid_r)
        two_r[...] = jnp.zeros_like(two_r)

    for g in range(groups):
        enc_v[g, :, LANES:] = jnp.ones((3 * gb, LANES), BF16)
        proc_v[g, :, LANES:] = jnp.ones((2 * hb, LANES), BF16)

    ld_enbr.wait()
    base = (me - 1) * gb
    row = lax.broadcasted_iota(jnp.int32, (3 * gb, rows), 0) + base
    for c in range(CHUNKS):
        counts = jnp.zeros((3 * gb, rows), F32)
        for j in range(enc_nbr.shape[0]):
            counts = counts + jnp.where(enc_nbr[j : j + 1, c * rows : (c + 1) * rows] == row, 1.0, 0.0)
        logs = jnp.log(jnp.maximum(counts, 1.0)) * math.log2(math.e)
        bias[c * rows : (c + 1) * rows, :] = jnp.where(counts > 0.0, logs, -1e30).T

    ld_grid.wait()
    ld_hidden.wait()
    ld_eqkv.wait()
    for ld in (ld_eout, ld_pqkv, ld_pout, ld_dnbr, ld_dqkv, ld_dout):
        ld.start()

    def enc_pairs(block, source):
        normed = layer_norm(source[...])
        enc_k[block * gb : (block + 1) * gb, :] = product(normed, enc_qkv[:, width : 2 * width]).astype(BF16)
        values = product(normed, enc_qkv[:, 2 * width :]).astype(BF16)
        for g in range(groups):
            enc_v[g, block * gb : (block + 1) * gb, :LANES] = values[:, g * LANES : (g + 1) * LANES]
        return normed

    grid_normed = enc_pairs(1, grid)
    enc_q[...] = (product(layer_norm(hidden[...]), enc_qkv[:, :width]) * scale).astype(BF16)

    @pl.when(has_l)
    def _():
        grid_up.wait_recv()

    @pl.when(has_r)
    def _():
        grid_down.wait_recv()

    enc_pairs(0, grid_l)
    enc_pairs(2, grid_r)

    masks = head_masks(rows, head_size)
    ld_eout.wait()
    one_copies = []
    for c in range(CHUNKS):
        part = slice(c * rows, (c + 1) * rows)
        for g in range(groups):
            lanes = slice(g * LANES, (g + 1) * LANES)
            mix[:, lanes] = attend_group(
                enc_q[part, lanes], enc_k[:, lanes], enc_v[g], bias[part, :], masks
            ).astype(BF16)
        one = (hidden[part, :].astype(F32) + product(mix[...], enc_out[...])).astype(BF16)
        hidden_one[part, :] = one
        norm_one[part, :] = layer_norm(one)
        copy = remote(norm_one.at[pl.ds(c * rows, rows)], norm_far.at[pl.ds(c * rows, rows)], 2 + c, far)
        copy.start()
        one_copies.append(copy)

    ld_min.start()
    ld_mout.start()
    ld_pqkv.wait()

    def proc_pairs(block, source):
        normed = source[...]
        proc_k[block * hb : (block + 1) * hb, :] = product(normed, proc_qkv[:, width : 2 * width]).astype(BF16)
        values = product(normed, proc_qkv[:, 2 * width :]).astype(BF16)
        for g in range(groups):
            proc_v[g, block * hb : (block + 1) * hb, :LANES] = values[:, g * LANES : (g + 1) * LANES]

    proc_q[...] = (product(norm_one[...], proc_qkv[:, :width]) * scale).astype(BF16)
    proc_pairs(0, norm_one)
    for copy in one_copies:
        copy.wait_recv()
    proc_pairs(1, norm_far)
    ld_pout.wait()
    two_copies = []
    for c in range(CHUNKS):
        part = slice(c * rows, (c + 1) * rows)
        for g in range(groups):
            lanes = slice(g * LANES, (g + 1) * LANES)
            mix[:, lanes] = attend_group(
                proc_q[part, lanes], proc_k[:, lanes], proc_v[g], None, masks
            ).astype(BF16)
        two = (hidden_one[part, :].astype(F32) + product(mix[...], proc_out[...])).astype(BF16)
        hidden_out[part, :] = two
        norm_two[part, :] = layer_norm(two)
        view = pl.ds(c * rows, rows)
        up = remote(norm_two.at[view], two_l.at[view], 2 + CHUNKS + 2 * c, me + 1)
        down = remote(norm_two.at[view], two_r.at[view], 3 + CHUNKS + 2 * c, me - 1)

        @pl.when(has_r)
        def _():
            up.start()

        @pl.when(has_l)
        def _():
            down.start()

        two_copies.append((up, down))
    store_hidden = pltpu.make_async_copy(hidden_out, hidden_out_hbm, store_sem.at[0])
    store_hidden.start()

    ld_dnbr.wait()
    ld_dqkv.wait()
    dec_q = product(grid_normed, dec_qkv[:, :width]).astype(BF16).astype(F32)
    dec_lists = dec_nbr[...] - (me - 1) * hb
    slots = dec_lists.shape[0]
    row = lax.broadcasted_iota(jnp.int32, (hb, gb), 0)

    def gather(block, source):
        hot = jnp.concatenate(
            [jnp.where(dec_lists[j : j + 1, :] == row + block * hb, 1.0, 0.0) for j in range(slots)], axis=1
        ).astype(BF16)
        return lax.dot_general(hot, source[...], (((0,), (0,)), ((), ())), preferred_element_type=F32)

    gathered = gather(1, norm_two)
    for up, down in two_copies:

        @pl.when(has_l)
        def _():
            up.wait_recv()

        @pl.when(has_r)
        def _():
            down.wait_recv()

    gathered = (gathered + gather(0, two_l) + gather(2, two_r)).astype(BF16)
    dec_k = product(gathered, dec_qkv[:, width : 2 * width]).astype(BF16).astype(F32)
    dec_v = product(gathered, dec_qkv[:, 2 * width :]).astype(BF16).astype(F32)
    wide = 2 * LANES
    same = (
        lax.broadcasted_iota(jnp.int32, (wide, wide), 0) // head_size
        == lax.broadcasted_iota(jnp.int32, (wide, wide), 1) // head_size
    )
    same = jnp.where(same, 1.0, 0.0).astype(BF16)
    terms = jnp.concatenate([dec_q] * slots, axis=0) * dec_k
    high = terms.astype(BF16)
    low = (terms - high.astype(F32)).astype(BF16)
    sums = [
        product(high[:, i : i + wide], same) + product(low[:, i : i + wide], same) for i in range(0, width, wide)
    ]
    scores = jnp.concatenate(sums, axis=1) * scale
    tops = scores[:gb]
    for j in range(1, slots):
        tops = jnp.maximum(tops, scores[j * gb : (j + 1) * gb])
    total = jnp.zeros((gb, width), F32)
    mixed = jnp.zeros((gb, width), F32)
    for j in range(slots):
        weight = jnp.exp2(scores[j * gb : (j + 1) * gb] - tops)
        total = total + weight
        mixed = mixed + weight * dec_v[j * gb : (j + 1) * gb]
    dec_mix = (mixed / total).astype(BF16)
    ld_dout.wait()
    grid_one = (grid[...].astype(F32) + product(dec_mix, dec_out[...])).astype(BF16)
    normed = layer_norm(grid_one)
    ld_min.wait()
    units = jax.nn.gelu(product(normed, mlp_in[...])).astype(BF16)
    ld_mout.wait()
    grid_out[...] = (grid_one.astype(F32) + product(units, mlp_out[...])).astype(BF16)
    store_grid = pltpu.make_async_copy(grid_out, grid_out_hbm, store_sem.at[1])
    store_grid.start()

    for copy in one_copies:
        copy.wait_send()

    @pl.when(has_r)
    def _():
        grid_up.wait_send()
        for up, _ in two_copies:
            up.wait_send()

    @pl.when(has_l)
    def _():
        grid_down.wait_send()
        for _, down in two_copies:
            down.wait_send()

    store_hidden.wait()
    store_grid.wait()


def local(*args):
    args = args[:2] + (args[2].T, args[3].T) + args[4:]
    grid, hidden = args[:2]
    gb, width = grid.shape
    hb = hidden.shape[0]
    groups = width // LANES
    n = lax.axis_size("nodes")
    vmem = [pltpu.VMEM(a.shape, a.dtype) for a in args]
    scratch = vmem + [
        pltpu.VMEM(grid.shape, BF16),
        pltpu.VMEM(hidden.shape, BF16),
        pltpu.VMEM(grid.shape, BF16),
        pltpu.VMEM(grid.shape, BF16),
        pltpu.VMEM((hb, 3 * gb), F32),
        pltpu.VMEM(hidden.shape, BF16),
        pltpu.VMEM((3 * gb, width), BF16),
        pltpu.VMEM((groups, 3 * gb, 2 * LANES), BF16),
        pltpu.VMEM(hidden.shape, BF16),
        pltpu.VMEM(hidden.shape, BF16),
        pltpu.VMEM(hidden.shape, BF16),
        pltpu.VMEM(hidden.shape, BF16),
        pltpu.VMEM((2 * hb, width), BF16),
        pltpu.VMEM((groups, 2 * hb, 2 * LANES), BF16),
        pltpu.VMEM(hidden.shape, BF16),
        pltpu.VMEM(hidden.shape, BF16),
        pltpu.VMEM(hidden.shape, BF16),
        pltpu.VMEM((hb // CHUNKS, width), BF16),
        pltpu.SemaphoreType.DMA((len(args),)),
        pltpu.SemaphoreType.DMA((2,)),
        pltpu.SemaphoreType.DMA((2 + 3 * CHUNKS,)),
        pltpu.SemaphoreType.DMA((2 + 3 * CHUNKS,)),
    ]
    return pl.pallas_call(
        functools.partial(kernel, n),
        out_shape=(jax.ShapeDtypeStruct(grid.shape, BF16), jax.ShapeDtypeStruct(hidden.shape, BF16)),
        in_specs=[pl.BlockSpec(memory_space=pl.ANY)] * len(args),
        out_specs=(pl.BlockSpec(memory_space=pl.ANY), pl.BlockSpec(memory_space=pl.ANY)),
        scratch_shapes=scratch,
        compiler_params=pltpu.CompilerParams(collective_id=0, has_side_effects=True, vmem_limit_bytes=60 * 2**20),
        name="layer",
    )(*args)


def solution(mesh):
    spread = P(("groups", "nodes"), None)
    return jax.shard_map(
        local,
        mesh=mesh,
        in_specs=(spread, spread, P("nodes", None), P("nodes", None)) + (P(),) * 8,
        out_specs=(spread, spread),
        check_vma=False,
    )
```

```python
import functools
import math

import jax
import jax.numpy as jnp
from jax import lax
from jax.experimental import pallas as pl
from jax.experimental.pallas import tpu as pltpu
from jax.sharding import PartitionSpec as P

HEADS = 16
EPSILON = 1e-05
LANES = 128
CHUNKS = 2
F32 = jnp.float32
BF16 = jnp.bfloat16
MESH = pl.DeviceIdType.MESH


def layer_norm(values):
    values = values.astype(F32)
    center = values - jnp.mean(values, axis=-1, keepdims=True)
    spread = jnp.mean(center * center, axis=-1, keepdims=True)
    return (center * lax.rsqrt(spread + EPSILON)).astype(BF16)


def product(left, right):
    return jnp.dot(left, right, preferred_element_type=F32)


def scores_of(left, right):
    return lax.dot_general(left, right, (((1,), (1,)), ((), ())), preferred_element_type=F32)


def head_masks(rows, head_size):
    lane = lax.broadcasted_iota(jnp.int32, (rows, LANES), 1)
    return [lane // head_size == h for h in range(LANES // head_size)]


def stacked_scores(queries, keys, masks):
    return scores_of(jnp.concatenate([jnp.where(m, queries, jnp.zeros_like(queries)) for m in masks], axis=0), keys)


def attend_rows(scores, values_ext, bias, masks):
    rows = scores.shape[0] // len(masks)
    num = den = None
    for h, mask in enumerate(masks):
        mine = scores[h * rows : (h + 1) * rows]
        if bias is not None:
            mine = mine + bias
        weights = jnp.exp2(mine - jnp.max(mine, axis=-1, keepdims=True)).astype(BF16)
        part = product(weights, values_ext)
        num = part[:, :LANES] if h == 0 else jnp.where(mask, part[:, :LANES], num)
        den = part[:, LANES:] if h == 0 else jnp.where(mask, part[:, LANES:], den)
    return num / den


def attend_all(queries, keys, values_ext, bias, masks, mix):
    groups = values_ext.shape[0]
    lanes = [slice(g * LANES, (g + 1) * LANES) for g in range(groups)]
    ahead = stacked_scores(queries[:, lanes[0]], keys[:, lanes[0]], masks)
    for g in range(groups):
        scores = ahead
        if g + 1 < groups:
            ahead = stacked_scores(queries[:, lanes[g + 1]], keys[:, lanes[g + 1]], masks)
        mix[:, lanes[g]] = attend_rows(scores, values_ext[g], bias, masks).astype(BF16)


def kernel(
    n,
    grid_hbm, hidden_hbm, enc_nbr_hbm, dec_nbr_hbm,
    enc_qkv_hbm, enc_out_hbm, proc_qkv_hbm, proc_out_hbm,
    dec_qkv_hbm, dec_out_hbm, mlp_in_hbm, mlp_out_hbm,
    grid_out, hidden_out,
    grid, hidden, enc_nbr, dec_nbr,
    enc_qkv, enc_out, proc_qkv, proc_out, dec_qkv, dec_out, mlp_in, mlp_out,
    grid_l, grid_r, bias, enc_q, enc_k, enc_v,
    hidden_one, norm_one, norm_far, proc_q, proc_k, proc_v,
    norm_two, two_l, two_r, mix,
    load_sem, send_sem, recv_sem,
):
    me = lax.axis_index("nodes")
    far = me + 1 - 2 * (me % 2)
    has_l = me > 0
    has_r = me < n - 1
    gb, width = grid.shape
    hb = hidden.shape[0]
    head_size = width // HEADS
    groups = width // LANES
    rows = hb // CHUNKS
    scale = math.log2(math.e) / math.sqrt(head_size)

    barrier = pltpu.get_barrier_semaphore()

    @pl.when(has_l)
    def _():
        pl.semaphore_signal(barrier, inc=1, device_id={"nodes": me - 1}, device_id_type=MESH)

    @pl.when(has_r)
    def _():
        pl.semaphore_signal(barrier, inc=1, device_id={"nodes": me + 1}, device_id_type=MESH)

    pairs = [
        (grid_hbm, grid), (hidden_hbm, hidden), (enc_nbr_hbm, enc_nbr), (enc_qkv_hbm, enc_qkv),
        (dec_nbr_hbm, dec_nbr), (enc_out_hbm, enc_out), (proc_qkv_hbm, proc_qkv), (proc_out_hbm, proc_out),
        (dec_qkv_hbm, dec_qkv), (dec_out_hbm, dec_out), (mlp_in_hbm, mlp_in), (mlp_out_hbm, mlp_out),
    ]
    loads = [pltpu.make_async_copy(s, d, load_sem.at[i]) for i, (s, d) in enumerate(pairs)]
    (ld_grid, ld_hidden, ld_enbr, ld_eqkv, ld_dnbr, ld_eout, ld_pqkv, ld_pout, ld_dqkv, ld_dout, ld_min, ld_mout) = loads
    for ld in (ld_grid, ld_hidden, ld_enbr, ld_eqkv):
        ld.start()

    def remote(src, dst, k, to):
        return pltpu.make_async_remote_copy(
            src_ref=src, dst_ref=dst, send_sem=send_sem.at[k], recv_sem=recv_sem.at[k],
            device_id={"nodes": to}, device_id_type=MESH,
        )

    grid_up = remote(grid_hbm, grid_l, 0, me + 1)
    grid_down = remote(grid_hbm, grid_r, 1, me - 1)

    pl.semaphore_wait(barrier, jnp.where(has_l, 1, 0) + jnp.where(has_r, 1, 0))

    @pl.when(has_r)
    def _():
        grid_up.start()

    @pl.when(has_l)
    def _():
        grid_down.start()

    @pl.when(jnp.logical_not(has_l))
    def _():
        grid_l[...] = jnp.zeros_like(grid_l)
        two_l[...] = jnp.zeros_like(two_l)

    @pl.when(jnp.logical_not(has_r))
    def _():
        grid_r[...] = jnp.zeros_like(grid_r)
        two_r[...] = jnp.zeros_like(two_r)

    for g in range(groups):
        enc_v[g, :, LANES:] = jnp.ones((3 * gb, LANES), BF16)
        proc_v[g, :, LANES:] = jnp.ones((2 * hb, LANES), BF16)

    ld_enbr.wait()
    base = (me - 1) * gb
    row = lax.broadcasted_iota(jnp.int32, (gb, rows), 0) + base
    for c in range(CHUNKS):
        for block in range(3):
            counts = jnp.zeros((gb, rows), F32)
            for j in range(enc_nbr.shape[0]):
                mine = enc_nbr[j : j + 1, c * rows : (c + 1) * rows] - block * gb
                counts = counts + jnp.where(mine == row, 1.0, 0.0)
            logs = jnp.log(jnp.maximum(counts, 1.0)) * math.log2(math.e)
            bias[c * rows : (c + 1) * rows, block * gb : (block + 1) * gb] = jnp.where(counts > 0.0, logs, -1e30).T

    ld_grid.wait()
    ld_hidden.wait()
    ld_eqkv.wait()
    for ld in (ld_eout, ld_pqkv, ld_pout, ld_dnbr, ld_dqkv, ld_dout):
        ld.start()

    def enc_pairs(block, source):
        normed = layer_norm(source[...])
        enc_k[block * gb : (block + 1) * gb, :] = product(normed, enc_qkv[:, width : 2 * width]).astype(BF16)
        values = product(normed, enc_qkv[:, 2 * width :]).astype(BF16)
        for g in range(groups):
            enc_v[g, block * gb : (block + 1) * gb, :LANES] = values[:, g * LANES : (g + 1) * LANES]
        return normed

    grid_normed = enc_pairs(1, grid)
    enc_q[...] = (product(layer_norm(hidden[...]), enc_qkv[:, :width]) * scale).astype(BF16)

    @pl.when(has_l)
    def _():
        grid_up.wait_recv()

    @pl.when(has_r)
    def _():
        grid_down.wait_recv()

    enc_pairs(0, grid_l)
    enc_pairs(2, grid_r)

    masks = head_masks(rows, head_size)
    ld_eout.wait()
    one_copies = []
    for c in range(CHUNKS):
        part = slice(c * rows, (c + 1) * rows)
        attend_all(enc_q.at[part], enc_k, enc_v, bias[part, :], masks, mix)
        one = (hidden[part, :].astype(F32) + product(mix[...], enc_out[...])).astype(BF16)
        hidden_one[part, :] = one
        norm_one[part, :] = layer_norm(one)
        copy = remote(norm_one.at[pl.ds(c * rows, rows)], norm_far.at[pl.ds(c * rows, rows)], 2 + c, far)
        copy.start()
        one_copies.append(copy)

    ld_min.start()
    ld_mout.start()
    ld_pqkv.wait()

    def proc_pairs(first, normed):
        place = slice(first, first + normed.shape[0])
        proc_k[place, :] = product(normed, proc_qkv[:, width : 2 * width]).astype(BF16)
        values = product(normed, proc_qkv[:, 2 * width :]).astype(BF16)
        for g in range(groups):
            proc_v[g, place, :LANES] = values[:, g * LANES : (g + 1) * LANES]

    proc_q[...] = (product(norm_one[...], proc_qkv[:, :width]) * scale).astype(BF16)
    proc_pairs(0, norm_one[...])
    for c, copy in enumerate(one_copies):
        copy.wait_recv()
        proc_pairs(hb + c * rows, norm_far[c * rows : (c + 1) * rows, :])
    ld_pout.wait()
    two_copies = []
    for c in range(CHUNKS):
        part = slice(c * rows, (c + 1) * rows)
        attend_all(proc_q.at[part], proc_k, proc_v, None, masks, mix)
        two = (hidden_one[part, :].astype(F32) + product(mix[...], proc_out[...])).astype(BF16)
        hidden_out[part, :] = two
        norm_two[part, :] = layer_norm(two)
        view = pl.ds(c * rows, rows)
        up = remote(norm_two.at[view], two_l.at[view], 2 + CHUNKS + 2 * c, me + 1)
        down = remote(norm_two.at[view], two_r.at[view], 3 + CHUNKS + 2 * c, me - 1)

        @pl.when(has_r)
        def _():
            up.start()

        @pl.when(has_l)
        def _():
            down.start()

        two_copies.append((up, down))

    ld_dnbr.wait()
    ld_dqkv.wait()
    dec_q = product(grid_normed, dec_qkv[:, :width]).astype(BF16).astype(F32)
    dec_lists = dec_nbr[...] - (me - 1) * hb
    slots = dec_lists.shape[0]
    row = lax.broadcasted_iota(jnp.int32, (hb, gb), 0)

    def gather(block, source):
        hot = jnp.concatenate(
            [jnp.where(dec_lists[j : j + 1, :] == row + block * hb, 1.0, 0.0) for j in range(slots)], axis=1
        ).astype(BF16)
        return lax.dot_general(hot, source[...], (((0,), (0,)), ((), ())), preferred_element_type=F32)

    gathered = gather(1, norm_two)
    for up, down in two_copies:

        @pl.when(has_l)
        def _():
            up.wait_recv()

        @pl.when(has_r)
        def _():
            down.wait_recv()

    gathered = (gathered + gather(0, two_l) + gather(2, two_r)).astype(BF16)
    dec_k = product(gathered, dec_qkv[:, width : 2 * width]).astype(BF16).astype(F32)
    dec_v = product(gathered, dec_qkv[:, 2 * width :]).astype(BF16).astype(F32)
    wide = 2 * LANES
    same = (
        lax.broadcasted_iota(jnp.int32, (wide, wide), 0) // head_size
        == lax.broadcasted_iota(jnp.int32, (wide, wide), 1) // head_size
    )
    same = jnp.where(same, 1.0, 0.0).astype(BF16)
    terms = jnp.concatenate([dec_q] * slots, axis=0) * dec_k
    high = terms.astype(BF16)
    low = (terms - high.astype(F32)).astype(BF16)
    sums = [
        product(high[:, i : i + wide], same) + product(low[:, i : i + wide], same) for i in range(0, width, wide)
    ]
    scores = jnp.concatenate(sums, axis=1) * scale
    tops = scores[:gb]
    for j in range(1, slots):
        tops = jnp.maximum(tops, scores[j * gb : (j + 1) * gb])
    total = jnp.zeros((gb, width), F32)
    mixed = jnp.zeros((gb, width), F32)
    for j in range(slots):
        weight = jnp.exp2(scores[j * gb : (j + 1) * gb] - tops)
        total = total + weight
        mixed = mixed + weight * dec_v[j * gb : (j + 1) * gb]
    dec_mix = (mixed / total).astype(BF16)
    ld_dout.wait()
    grid_one = (grid[...].astype(F32) + product(dec_mix, dec_out[...])).astype(BF16)
    normed = layer_norm(grid_one)
    ld_min.wait()
    ld_mout.wait()
    ahead = product(normed, mlp_in[:, :width])
    total = grid_one.astype(F32)
    for i in range(0, mlp_in.shape[1], width):
        now = ahead
        if i + width < mlp_in.shape[1]:
            ahead = product(normed, mlp_in[:, i + width : i + 2 * width])
        total = total + product(jax.nn.gelu(now).astype(BF16), mlp_out[i : i + width, :])
    grid_out[...] = total.astype(BF16)

    for copy in one_copies:
        copy.wait_send()

    @pl.when(has_r)
    def _():
        grid_up.wait_send()
        for up, _ in two_copies:
            up.wait_send()

    @pl.when(has_l)
    def _():
        grid_down.wait_send()
        for _, down in two_copies:
            down.wait_send()


def local(*args):
    args = args[:2] + (args[2].T, args[3].T) + args[4:]
    grid, hidden = args[:2]
    gb, width = grid.shape
    hb = hidden.shape[0]
    groups = width // LANES
    n = lax.axis_size("nodes")
    vmem = [pltpu.VMEM(a.shape, a.dtype) for a in args]
    scratch = vmem + [
        pltpu.VMEM(grid.shape, BF16),
        pltpu.VMEM(grid.shape, BF16),
        pltpu.VMEM((hb, 3 * gb), F32),
        pltpu.VMEM(hidden.shape, BF16),
        pltpu.VMEM((3 * gb, width), BF16),
        pltpu.VMEM((groups, 3 * gb, 2 * LANES), BF16),
        pltpu.VMEM(hidden.shape, BF16),
        pltpu.VMEM(hidden.shape, BF16),
        pltpu.VMEM(hidden.shape, BF16),
        pltpu.VMEM(hidden.shape, BF16),
        pltpu.VMEM((2 * hb, width), BF16),
        pltpu.VMEM((groups, 2 * hb, 2 * LANES), BF16),
        pltpu.VMEM(hidden.shape, BF16),
        pltpu.VMEM(hidden.shape, BF16),
        pltpu.VMEM(hidden.shape, BF16),
        pltpu.VMEM((hb // CHUNKS, width), BF16),
        pltpu.SemaphoreType.DMA((len(args),)),
        pltpu.SemaphoreType.DMA((2 + 3 * CHUNKS,)),
        pltpu.SemaphoreType.DMA((2 + 3 * CHUNKS,)),
    ]
    args = [pltpu.with_memory_space_constraint(a, pltpu.HBM) for a in args]
    mid = pl.pallas_call(
        functools.partial(kernel, n),
        out_shape=(jax.ShapeDtypeStruct(grid.shape, BF16), jax.ShapeDtypeStruct(hidden.shape, BF16)),
        in_specs=[pl.BlockSpec(memory_space=pl.ANY)] * len(args),
        out_specs=(pl.BlockSpec(memory_space=pltpu.VMEM), pl.BlockSpec(memory_space=pltpu.VMEM)),
        scratch_shapes=scratch,
        compiler_params=pltpu.CompilerParams(collective_id=0, has_side_effects=True, vmem_limit_bytes=40 * 2**20),
        name="layer",
    )(*args)
    return pl.pallas_call(
        finish,
        out_shape=(jax.ShapeDtypeStruct(grid.shape, BF16), jax.ShapeDtypeStruct(hidden.shape, BF16)),
        in_specs=[pl.BlockSpec(memory_space=pl.ANY)] * 2,
        out_specs=(pl.BlockSpec(memory_space=pl.ANY), pl.BlockSpec(memory_space=pl.ANY)),
        scratch_shapes=[pltpu.SemaphoreType.DMA((2,))],
        compiler_params=pltpu.CompilerParams(vmem_limit_bytes=2**20),
        name="finish",
    )(*mid)


def finish(grid_mid, hidden_mid, grid_out, hidden_out, sem):
    one = pltpu.make_async_copy(grid_mid, grid_out, sem.at[0])
    two = pltpu.make_async_copy(hidden_mid, hidden_out, sem.at[1])
    one.start()
    two.start()
    one.wait()
    two.wait()


def solution(mesh):
    spread = P(("groups", "nodes"), None)
    return jax.shard_map(
        local,
        mesh=mesh,
        in_specs=(spread, spread, P("nodes", None), P("nodes", None)) + (P(),) * 8,
        out_specs=(spread, spread),
        check_vma=False,
    )
```

```python
import functools
import math

import jax
import jax.numpy as jnp
from jax import lax
from jax.experimental import pallas as pl
from jax.experimental.pallas import tpu as pltpu
from jax.sharding import PartitionSpec as P

HEADS = 16
EPSILON = 1e-05
LANES = 128
CHUNKS = 2
F32 = jnp.float32
BF16 = jnp.bfloat16
MESH = pl.DeviceIdType.MESH


def layer_norm(values):
    values = values.astype(F32)
    center = values - jnp.mean(values, axis=-1, keepdims=True)
    spread = jnp.mean(center * center, axis=-1, keepdims=True)
    return (center * lax.rsqrt(spread + EPSILON)).astype(BF16)


def product(left, right):
    return jnp.dot(left, right, preferred_element_type=F32)


def scores_of(left, right):
    return lax.dot_general(left, right, (((1,), (1,)), ((), ())), preferred_element_type=F32)


def head_masks(rows, head_size):
    lane = lax.broadcasted_iota(jnp.int32, (rows, LANES), 1)
    return [lane // head_size == h for h in range(LANES // head_size)]


def stacked_scores(queries, keys, masks):
    return scores_of(jnp.concatenate([jnp.where(m, queries, jnp.zeros_like(queries)) for m in masks], axis=0), keys)


def attend_rows(scores, values_ext, bias, masks):
    rows = scores.shape[0] // len(masks)
    num = den = None
    for h, mask in enumerate(masks):
        mine = scores[h * rows : (h + 1) * rows]
        if bias is not None:
            mine = mine + bias
        weights = jnp.exp2(mine - jnp.max(mine, axis=-1, keepdims=True)).astype(BF16)
        part = product(weights, values_ext)
        num = part[:, :LANES] if h == 0 else jnp.where(mask, part[:, :LANES], num)
        den = part[:, LANES:] if h == 0 else jnp.where(mask, part[:, LANES:], den)
    return num / den


def attend_all(queries, keys, values_ext, bias, masks, mix):
    groups = values_ext.shape[0]
    lanes = [slice(g * LANES, (g + 1) * LANES) for g in range(groups)]
    ahead = stacked_scores(queries[:, lanes[0]], keys[:, lanes[0]], masks)
    for g in range(groups):
        scores = ahead
        if g + 1 < groups:
            ahead = stacked_scores(queries[:, lanes[g + 1]], keys[:, lanes[g + 1]], masks)
        mix[:, lanes[g]] = attend_rows(scores, values_ext[g], bias, masks).astype(BF16)


def kernel(
    n,
    grid_hbm, hidden_hbm, enc_nbr_hbm, dec_nbr_hbm,
    enc_qkv_hbm, enc_out_hbm, proc_qkv_hbm, proc_out_hbm,
    dec_qkv_hbm, dec_out_hbm, mlp_in_hbm, mlp_out_hbm,
    grid_out, hidden_out,
    grid, hidden, enc_nbr, dec_nbr,
    enc_qkv, enc_out, proc_qkv, proc_out, dec_qkv, dec_out, mlp_in, mlp_out,
    grid_l, grid_r, bias, enc_q, enc_k, enc_v,
    hidden_one, norm_one, norm_far, proc_q, proc_k, proc_v,
    norm_two, two_l, two_r, mix,
    load_sem, send_sem, recv_sem,
):
    me = lax.axis_index("nodes")
    far = me + 1 - 2 * (me % 2)
    has_l = me > 0
    has_r = me < n - 1
    gb, width = grid.shape
    hb = hidden.shape[0]
    head_size = width // HEADS
    groups = width // LANES
    rows = hb // CHUNKS
    scale = math.log2(math.e) / math.sqrt(head_size)

    barrier = pltpu.get_barrier_semaphore()

    @pl.when(has_l)
    def _():
        pl.semaphore_signal(barrier, inc=1, device_id={"nodes": me - 1}, device_id_type=MESH)

    @pl.when(has_r)
    def _():
        pl.semaphore_signal(barrier, inc=1, device_id={"nodes": me + 1}, device_id_type=MESH)

    pairs = [
        (grid_hbm, grid), (hidden_hbm, hidden), (enc_nbr_hbm, enc_nbr), (enc_qkv_hbm, enc_qkv),
        (dec_nbr_hbm, dec_nbr), (enc_out_hbm, enc_out), (proc_qkv_hbm, proc_qkv), (proc_out_hbm, proc_out),
        (dec_qkv_hbm, dec_qkv), (dec_out_hbm, dec_out), (mlp_in_hbm, mlp_in), (mlp_out_hbm, mlp_out),
    ]
    loads = [pltpu.make_async_copy(s, d, load_sem.at[i]) for i, (s, d) in enumerate(pairs)]
    (ld_grid, ld_hidden, ld_enbr, ld_eqkv, ld_dnbr, ld_eout, ld_pqkv, ld_pout, ld_dqkv, ld_dout, ld_min, ld_mout) = loads
    for ld in (ld_grid, ld_hidden, ld_enbr, ld_eqkv):
        ld.start()

    def remote(src, dst, k, to):
        return pltpu.make_async_remote_copy(
            src_ref=src, dst_ref=dst, send_sem=send_sem.at[k], recv_sem=recv_sem.at[k],
            device_id={"nodes": to}, device_id_type=MESH,
        )

    grid_up = remote(grid_hbm, grid_l, 0, me + 1)
    grid_down = remote(grid_hbm, grid_r, 1, me - 1)

    pl.semaphore_wait(barrier, jnp.where(has_l, 1, 0) + jnp.where(has_r, 1, 0))

    @pl.when(has_r)
    def _():
        grid_up.start()

    @pl.when(has_l)
    def _():
        grid_down.start()

    @pl.when(jnp.logical_not(has_l))
    def _():
        grid_l[...] = jnp.zeros_like(grid_l)
        two_l[...] = jnp.zeros_like(two_l)

    @pl.when(jnp.logical_not(has_r))
    def _():
        grid_r[...] = jnp.zeros_like(grid_r)
        two_r[...] = jnp.zeros_like(two_r)

    for g in range(groups):
        enc_v[g, :, LANES:] = jnp.ones((3 * gb, LANES), BF16)
        proc_v[g, :, LANES:] = jnp.ones((2 * hb, LANES), BF16)

    ld_enbr.wait()
    base = (me - 1) * gb
    row = lax.broadcasted_iota(jnp.int32, (gb, rows), 0) + base
    for c in range(CHUNKS):
        for block in range(3):
            counts = jnp.zeros((gb, rows), F32)
            for j in range(enc_nbr.shape[0]):
                mine = enc_nbr[j : j + 1, c * rows : (c + 1) * rows] - block * gb
                counts = counts + jnp.where(mine == row, 1.0, 0.0)
            logs = jnp.log(jnp.maximum(counts, 1.0)) * math.log2(math.e)
            bias[c * rows : (c + 1) * rows, block * gb : (block + 1) * gb] = jnp.where(counts > 0.0, logs, -1e30).T

    ld_grid.wait()
    ld_hidden.wait()
    ld_eqkv.wait()
    for ld in (ld_eout, ld_pqkv, ld_pout, ld_dnbr, ld_dqkv, ld_dout):
        ld.start()

    def enc_pairs(block, source):
        normed = layer_norm(source[...])
        enc_k[block * gb : (block + 1) * gb, :] = product(normed, enc_qkv[:, width : 2 * width]).astype(BF16)
        values = product(normed, enc_qkv[:, 2 * width :]).astype(BF16)
        for g in range(groups):
            enc_v[g, block * gb : (block + 1) * gb, :LANES] = values[:, g * LANES : (g + 1) * LANES]
        return normed

    grid_normed = enc_pairs(1, grid)
    enc_q[...] = (product(layer_norm(hidden[...]), enc_qkv[:, :width]) * scale).astype(BF16)

    @pl.when(has_l)
    def _():
        grid_up.wait_recv()

    @pl.when(has_r)
    def _():
        grid_down.wait_recv()

    enc_pairs(0, grid_l)
    enc_pairs(2, grid_r)

    masks = head_masks(rows, head_size)
    ld_eout.wait()
    one_copies = []
    for c in range(CHUNKS):
        part = slice(c * rows, (c + 1) * rows)
        attend_all(enc_q.at[part], enc_k, enc_v, bias[part, :], masks, mix)
        one = (hidden[part, :].astype(F32) + product(mix[...], enc_out[...])).astype(BF16)
        hidden_one[part, :] = one
        norm_one[part, :] = layer_norm(one)
        copy = remote(norm_one.at[pl.ds(c * rows, rows)], norm_far.at[pl.ds(c * rows, rows)], 2 + c, far)
        copy.start()
        one_copies.append(copy)

    ld_min.start()
    ld_mout.start()
    ld_pqkv.wait()

    def proc_pairs(first, normed):
        place = slice(first, first + normed.shape[0])
        proc_k[place, :] = product(normed, proc_qkv[:, width : 2 * width]).astype(BF16)
        values = product(normed, proc_qkv[:, 2 * width :]).astype(BF16)
        for g in range(groups):
            proc_v[g, place, :LANES] = values[:, g * LANES : (g + 1) * LANES]

    proc_q[...] = (product(norm_one[...], proc_qkv[:, :width]) * scale).astype(BF16)
    proc_pairs(0, norm_one[...])
    for c, copy in enumerate(one_copies):
        copy.wait_recv()
        proc_pairs(hb + c * rows, norm_far[c * rows : (c + 1) * rows, :])
    ld_pout.wait()
    two_copies = []
    for c in range(CHUNKS):
        part = slice(c * rows, (c + 1) * rows)
        attend_all(proc_q.at[part], proc_k, proc_v, None, masks, mix)
        two = (hidden_one[part, :].astype(F32) + product(mix[...], proc_out[...])).astype(BF16)
        hidden_out[part, :] = two
        norm_two[part, :] = layer_norm(two)
        view = pl.ds(c * rows, rows)
        up = remote(norm_two.at[view], two_l.at[view], 2 + CHUNKS + 2 * c, me + 1)
        down = remote(norm_two.at[view], two_r.at[view], 3 + CHUNKS + 2 * c, me - 1)

        @pl.when(has_r)
        def _():
            up.start()

        @pl.when(has_l)
        def _():
            down.start()

        two_copies.append((up, down))

    ld_dnbr.wait()
    ld_dqkv.wait()
    dec_q = product(grid_normed, dec_qkv[:, :width]).astype(BF16).astype(F32)
    dec_lists = dec_nbr[...] - (me - 1) * hb
    slots = dec_lists.shape[0]
    row = lax.broadcasted_iota(jnp.int32, (hb, gb), 0)

    def hot(block):
        per_slot = [
            jnp.where(dec_lists[j : j + 1, :] == row + block * hb, 1.0, 0.0).T for j in range(slots)
        ]
        return jnp.concatenate(per_slot, axis=0).astype(BF16)

    hot_l, hot_r = hot(0), hot(2)
    gathered = product(hot(1), norm_two[...])
    for c, (up, down) in enumerate(two_copies):

        @pl.when(has_l)
        def _():
            up.wait_recv()

        @pl.when(has_r)
        def _():
            down.wait_recv()

        part = slice(c * rows, (c + 1) * rows)
        picks = jnp.concatenate([hot_l[:, part], hot_r[:, part]], axis=1)
        gathered = gathered + product(picks, jnp.concatenate([two_l[part, :], two_r[part, :]], axis=0))
    gathered = gathered.astype(BF16)
    dec_k = product(gathered, dec_qkv[:, width : 2 * width]).astype(BF16).astype(F32)
    dec_v = product(gathered, dec_qkv[:, 2 * width :]).astype(BF16).astype(F32)
    wide = 2 * LANES
    same = (
        lax.broadcasted_iota(jnp.int32, (wide, wide), 0) // head_size
        == lax.broadcasted_iota(jnp.int32, (wide, wide), 1) // head_size
    )
    same = jnp.where(same, 1.0, 0.0).astype(BF16)
    terms = jnp.concatenate([dec_q] * slots, axis=0) * dec_k
    high = terms.astype(BF16)
    low = (terms - high.astype(F32)).astype(BF16)
    sums = [
        product(high[:, i : i + wide], same) + product(low[:, i : i + wide], same) for i in range(0, width, wide)
    ]
    scores = jnp.concatenate(sums, axis=1) * scale
    tops = scores[:gb]
    for j in range(1, slots):
        tops = jnp.maximum(tops, scores[j * gb : (j + 1) * gb])
    total = jnp.zeros((gb, width), F32)
    mixed = jnp.zeros((gb, width), F32)
    for j in range(slots):
        weight = jnp.exp2(scores[j * gb : (j + 1) * gb] - tops)
        total = total + weight
        mixed = mixed + weight * dec_v[j * gb : (j + 1) * gb]
    dec_mix = (mixed / total).astype(BF16)
    ld_dout.wait()
    grid_one = (grid[...].astype(F32) + product(dec_mix, dec_out[...])).astype(BF16)
    normed = layer_norm(grid_one)
    ld_min.wait()
    ld_mout.wait()
    ahead = product(normed, mlp_in[:, :width])
    total = grid_one.astype(F32)
    for i in range(0, mlp_in.shape[1], width):
        now = ahead
        if i + width < mlp_in.shape[1]:
            ahead = product(normed, mlp_in[:, i + width : i + 2 * width])
        total = total + product(jax.nn.gelu(now).astype(BF16), mlp_out[i : i + width, :])
    grid_out[...] = total.astype(BF16)

    for copy in one_copies:
        copy.wait_send()

    @pl.when(has_r)
    def _():
        grid_up.wait_send()
        for up, _ in two_copies:
            up.wait_send()

    @pl.when(has_l)
    def _():
        grid_down.wait_send()
        for _, down in two_copies:
            down.wait_send()


def local(*args):
    args = args[:2] + (args[2].T, args[3].T) + args[4:]
    grid, hidden = args[:2]
    gb, width = grid.shape
    hb = hidden.shape[0]
    groups = width // LANES
    n = lax.axis_size("nodes")
    vmem = [pltpu.VMEM(a.shape, a.dtype) for a in args]
    scratch = vmem + [
        pltpu.VMEM(grid.shape, BF16),
        pltpu.VMEM(grid.shape, BF16),
        pltpu.VMEM((hb, 3 * gb), F32),
        pltpu.VMEM(hidden.shape, BF16),
        pltpu.VMEM((3 * gb, width), BF16),
        pltpu.VMEM((groups, 3 * gb, 2 * LANES), BF16),
        pltpu.VMEM(hidden.shape, BF16),
        pltpu.VMEM(hidden.shape, BF16),
        pltpu.VMEM(hidden.shape, BF16),
        pltpu.VMEM(hidden.shape, BF16),
        pltpu.VMEM((2 * hb, width), BF16),
        pltpu.VMEM((groups, 2 * hb, 2 * LANES), BF16),
        pltpu.VMEM(hidden.shape, BF16),
        pltpu.VMEM(hidden.shape, BF16),
        pltpu.VMEM(hidden.shape, BF16),
        pltpu.VMEM((hb // CHUNKS, width), BF16),
        pltpu.SemaphoreType.DMA((len(args),)),
        pltpu.SemaphoreType.DMA((2 + 3 * CHUNKS,)),
        pltpu.SemaphoreType.DMA((2 + 3 * CHUNKS,)),
    ]
    args = [pltpu.with_memory_space_constraint(a, pltpu.HBM) for a in args]
    mid = pl.pallas_call(
        functools.partial(kernel, n),
        out_shape=(jax.ShapeDtypeStruct(grid.shape, BF16), jax.ShapeDtypeStruct(hidden.shape, BF16)),
        in_specs=[pl.BlockSpec(memory_space=pl.ANY)] * len(args),
        out_specs=(pl.BlockSpec(memory_space=pltpu.VMEM), pl.BlockSpec(memory_space=pltpu.VMEM)),
        scratch_shapes=scratch,
        compiler_params=pltpu.CompilerParams(collective_id=0, has_side_effects=True, vmem_limit_bytes=40 * 2**20),
        name="layer",
    )(*args)
    return pl.pallas_call(
        finish,
        out_shape=(jax.ShapeDtypeStruct(grid.shape, BF16), jax.ShapeDtypeStruct(hidden.shape, BF16)),
        in_specs=[pl.BlockSpec(memory_space=pl.ANY)] * 2,
        out_specs=(pl.BlockSpec(memory_space=pl.ANY), pl.BlockSpec(memory_space=pl.ANY)),
        scratch_shapes=[pltpu.SemaphoreType.DMA((2,))],
        compiler_params=pltpu.CompilerParams(vmem_limit_bytes=2**20),
        name="finish",
    )(*mid)


def finish(grid_mid, hidden_mid, grid_out, hidden_out, sem):
    one = pltpu.make_async_copy(grid_mid, grid_out, sem.at[0])
    two = pltpu.make_async_copy(hidden_mid, hidden_out, sem.at[1])
    one.start()
    two.start()
    one.wait()
    two.wait()


def solution(mesh):
    spread = P(("groups", "nodes"), None)
    return jax.shard_map(
        local,
        mesh=mesh,
        in_specs=(spread, spread, P("nodes", None), P("nodes", None)) + (P(),) * 8,
        out_specs=(spread, spread),
        check_vma=False,
    )
```
